32 devices in a mesh: seq: 16 (over z, y, x), head: 2 (over core).
Axes of the slice: x: 2, y: 2, z: 4, core: 2. Of those that a mesh axis runs over, the one named last changes fastest.
Arguments:
- queries: bfloat16 [4096, 128], P('seq'), may hold values from -6 to 6
- keys: bfloat16 [4096, 128], P('seq'), may hold values from -6 to 6
- values: bfloat16 [4096, 2048], P('seq', 'head'), may hold values from -6 to 6
- out_grad: bfloat16 [4096, 2048], P('seq', 'head'), may hold values from -6 to 6
- raw_trans: float32 [16, 128, 128], P('seq'), may hold values from -1 to 1, as said below
Outputs:
- outputs: bfloat16 [4096, 2048], P('seq', 'head')
- grad_queries: bfloat16 [4096, 128], P(('seq', 'head'))
- grad_keys: bfloat16 [4096, 128], P(('seq', 'head'))
- grad_values: bfloat16 [4096, 2048], P('seq', 'head')
- grad_trans: float32 [128, 16, 128], P('head', 'seq')
The draws below stay inside these ranges and needn't reach their ends.
Inputs may be any that keep to these rules, and one draw needn't show every extreme that they name: Every block of raw_trans has a positive diagonal.
All inputs are finite; a program needn't handle non-finite values.
Results may differ from the reference program's by a relative error of at most 0.019.
Values may be sent and summed in bfloat16 or wider, within the bound.
A program may use at most 64 MiB of HBM per device.

```python
import math
import jax
import jax.numpy as jnp
from jax import lax

STATE_ROWS = 128
H = 8
P_SIZE = 256
L = 256
TOKENS = 4096
BLOCK_COUNT = 16


def draw_raw_trans(key, part):
    parallel_lanes = jax.random.split(key, 8)
    order = jax.random.permutation(parallel_lanes[0], STATE_ROWS)
    slow_states = order < STATE_ROWS // 2
    slow_rate = jnp.exp(jax.random.uniform(parallel_lanes[1], (STATE_ROWS,), jnp.float32, math.log(0.001), math.log(0.02)))
    fast_rate = jnp.exp(jax.random.uniform(parallel_lanes[2], (STATE_ROWS,), jnp.float32, math.log(0.3), math.log(1.5)))
    rates = jnp.where(slow_states, slow_rate, fast_rate)
    jitter = jnp.exp(jax.random.uniform(parallel_lanes[3], (BLOCK_COUNT, STATE_ROWS), jnp.float32, math.log(0.5), math.log(2.0)))
    recurrent_block = jax.random.randint(parallel_lanes[4], (BLOCK_COUNT, 1), 0, 16) == 0
    recurrent_state = jax.random.randint(parallel_lanes[5], (BLOCK_COUNT, STATE_ROWS), 0, 2) == 0
    sequence_cutter = jax.random.uniform(parallel_lanes[6], (BLOCK_COUNT, STATE_ROWS), jnp.float32, 0.5, 0.8)
    decay_factor = jnp.where(recurrent_block & recurrent_state, sequence_cutter, 1.0)
    diagonal = jnp.exp(-rates[None, :] * jitter) * decay_factor
    noise = jax.random.truncated_normal(parallel_lanes[7], -4.0, 4.0, (BLOCK_COUNT, STATE_ROWS, STATE_ROWS), jnp.float32)
    skewed = (noise - jnp.swapaxes(noise, 1, 2)) * (0.075 / math.sqrt(2.0 * STATE_ROWS))
    indices = jnp.arange(STATE_ROWS)
    on_diagonal = indices[:, None] == indices[None, :]
    return jnp.where(on_diagonal[None], diagonal[:, None, :], skewed).astype(jnp.float32)


def steps_of(own_key, dims, cuts, smallest, top_value):
    def one(axis_at, parts):
        steps = jax.random.uniform(jax.random.fold_in(jax.random.fold_in(own_key, 6), axis_at), (parts,), jnp.float32, smallest / len(cuts), top_value / len(cuts))
        return jnp.repeat(jnp.exp(steps), dims[axis_at] // parts).reshape((-1,) + (1,) * (len(dims) - axis_at - 1))

    factor_of = one(*cuts[0])
    for cut in cuts[1:]:
        factor_of = factor_of * one(*cut)
    return factor_of


def scatter_about(own_key, extent, spread, limit, shards=(), held_as=jnp.bfloat16):
    entries = jax.random.normal(own_key, extent, jnp.float32) * spread
    if len(shards) > 0:
        entries = steps_of(own_key, extent, shards, -0.22, 0.18) * entries
    return jnp.clip(entries, min=-limit, max=limit).astype(held_as)


def setup_inputs(seed: int = 0) -> dict:
    splits = jax.random.split(jax.random.key(seed), 6)
    return {
        "queries": scatter_about(splits[0], (TOKENS, STATE_ROWS), 1.0, 6.0, ((0, 16),)),
        "keys": scatter_about(splits[1], (TOKENS, STATE_ROWS), 1.0, 6.0, ((0, 16),)),
        "values": scatter_about(splits[2], (TOKENS, H * P_SIZE), 1.0, 6.0, ((0, 16), (1, 2))),
        "out_grad": scatter_about(splits[3], (TOKENS, H * P_SIZE), 1.0, 6.0, ((0, 16), (1, 2))),
        "raw_trans": draw_raw_trans(jax.random.fold_in(splits[5], 71), 0),
    }


PRECISE = lax.Precision.HIGHEST

def normalize_blocks(raw):
    count = raw.shape[-1]
    vector = jnp.ones(raw.shape[:-1], jnp.float32) / math.sqrt(count)
    for repeat in range(6):
        product = jnp.einsum('cij,cj->ci', raw, vector, precision=PRECISE)
        returned = jnp.einsum('cji,cj->ci', raw, product, precision=PRECISE)
        vector = returned / jnp.sqrt(lax.optimization_barrier(jnp.sum(returned * returned, axis=-1, keepdims=True)))
    product = jnp.einsum('cij,cj->ci', raw, vector, precision=PRECISE)
    spectral = jnp.sqrt(lax.optimization_barrier(jnp.sum(product * product, axis=-1)))
    return raw / spectral[:, None, None]

def reference(queries, keys, values, out_grad, raw_trans):
    attn_scale = 0.5 / math.sqrt(STATE_ROWS * L)
    transition = normalize_blocks(raw_trans)
    col_count = H * P_SIZE
    query_blocks = queries.reshape(BLOCK_COUNT, L, STATE_ROWS)
    key_blocks = keys.reshape(BLOCK_COUNT, L, STATE_ROWS)
    value_blocks = values.reshape(BLOCK_COUNT, L, col_count)
    grad_blocks = out_grad.reshape(BLOCK_COUNT, L, col_count)
    causal = jnp.arange(L)[:, None] >= jnp.arange(L)[None, :]

    def forward_step(state_now, pieces):
        matrix, query_rows, key_rows, value_rows = pieces
        state_low = state_now.astype(jnp.bfloat16)
        scores = jnp.dot(query_rows, key_rows.T, preferred_element_type=jnp.float32)
        weights = jnp.where(causal, attn_scale * scores, 0.0).astype(jnp.bfloat16)
        output = attn_scale * jnp.dot(query_rows, state_low, preferred_element_type=jnp.float32) + jnp.dot(weights, value_rows, preferred_element_type=jnp.float32)
        update = jnp.dot(key_rows.T, value_rows, preferred_element_type=jnp.float32)
        state_next = jnp.dot(matrix, state_now, precision=PRECISE) + update
        return (state_next, (output.astype(jnp.bfloat16), state_low, weights))
    final_state, (outputs, state_lows, weight_blocks) = lax.scan(forward_step, jnp.zeros((STATE_ROWS, col_count), jnp.float32), (transition, query_blocks, key_blocks, value_blocks))

    def backward_step(carried, pieces):
        matrix, query_rows, key_rows, value_rows, grad_rows, state_low, weights = pieces
        carried_low = carried.astype(jnp.bfloat16)
        grad_value = jnp.dot(weights.T, grad_rows, preferred_element_type=jnp.float32) + jnp.dot(key_rows, carried_low, preferred_element_type=jnp.float32)
        heads_grad = grad_rows.reshape(L, H, P_SIZE).astype(jnp.float32)
        heads_value = value_rows.reshape(L, H, P_SIZE).astype(jnp.float32)
        dscore = jnp.einsum('lhp,mhp->hlm', heads_grad, heads_value)
        score_grad = jnp.where(causal[None], attn_scale * dscore, 0.0).astype(jnp.bfloat16)
        grad_query = attn_scale * jnp.dot(grad_rows, state_low.T, preferred_element_type=jnp.float32) + jnp.einsum('hlm,mn->ln', score_grad.astype(jnp.float32), key_rows.astype(jnp.float32))
        grad_key = jnp.dot(value_rows, carried_low.T, preferred_element_type=jnp.float32) + jnp.einsum('hlm,ln->mn', score_grad.astype(jnp.float32), query_rows.astype(jnp.float32))
        grad_matrix = jnp.dot(carried_low, state_low.T, preferred_element_type=jnp.float32)
        carried_next = attn_scale * jnp.dot(query_rows.T, grad_rows, preferred_element_type=jnp.float32) + jnp.dot(matrix.T, carried, precision=PRECISE)
        return (carried_next, (grad_query.astype(jnp.bfloat16), grad_key.astype(jnp.bfloat16), grad_value.astype(jnp.bfloat16), grad_matrix))
    first_grad, (grad_q, grad_k, grad_v, grad_m) = lax.scan(backward_step, jnp.zeros((STATE_ROWS, col_count), jnp.float32), (transition, query_blocks, key_blocks, value_blocks, grad_blocks, state_lows, weight_blocks), reverse=True)
    return (outputs.reshape(BLOCK_COUNT * L, col_count), grad_q.reshape(BLOCK_COUNT * L, STATE_ROWS), grad_k.reshape(BLOCK_COUNT * L, STATE_ROWS), grad_v.reshape(BLOCK_COUNT * L, col_count), jnp.transpose(grad_m, (1, 0, 2)))
```

```python
import functools
import math

import jax
import jax.numpy as jnp
from jax import lax
from jax.experimental import pallas as pl
from jax.experimental.pallas import tpu as pltpu
from jax.sharding import PartitionSpec as P

STATE_ROWS = 128
P_SIZE = 256
L = 256

F32 = jnp.float32
BF16 = jnp.bfloat16
MESH = pl.DeviceIdType.MESH
NN = (((1,), (0,)), ((), ()))
NT = (((1,), (1,)), ((), ()))
TN = (((0,), (0,)), ((), ()))


def mm(a, b, dims):
    return lax.dot_general(a, b, dims, preferred_element_type=F32)


def normalized(raw):
    rows, count = raw.shape
    vector = jnp.full((1, count), 1.0 / math.sqrt(count), F32)
    for _ in range(6):
        product = jnp.sum(raw * vector, axis=1, keepdims=True)
        returned = jnp.sum(raw * product, axis=0, keepdims=True)
        vector = returned / jnp.sqrt(jnp.sum(returned * returned, axis=1, keepdims=True))
    product = jnp.sum(raw * vector, axis=1, keepdims=True)
    return raw / jnp.sqrt(jnp.sum(product * product, axis=0, keepdims=True))


def kernel(
    n,
    nh,
    n_own,
    rows,
    q_ref,
    k_ref,
    v_ref,
    dy_ref,
    raw_ref,
    out_ref,
    gq_ref,
    gk_ref,
    gv_ref,
    gt_ref,
    u_src,
    u_all,
    m_src,
    m_all,
    s_src,
    s_all,
    av_acc,
    ady_acc,
    gqk_part,
    gqk_all,
    gt_part,
    gt_all,
    u_send,
    u_recv,
    m_send,
    m_recv,
    s_send,
    s_recv,
    h_send,
    h_recv,
):
    me = lax.axis_index("seq")
    core = lax.axis_index("head")
    tokens, states = q_ref.shape
    cols = v_ref.shape[1]
    heads_here = cols // P_SIZE
    scale = 0.5 / math.sqrt(STATE_ROWS * L)

    def peer(i):
        return lax.rem(me + i, n)

    def partner(i):
        return lax.rem(core + i, nh)

    barrier = pltpu.get_barrier_semaphore()

    def greet(i, carry):
        pl.semaphore_signal(
            barrier, inc=1, device_id={"seq": peer(i), "head": core}, device_id_type=MESH
        )
        return carry

    def greet_head(i, carry):
        pl.semaphore_signal(
            barrier, inc=1, device_id={"seq": me, "head": partner(i)}, device_id_type=MESH
        )
        return carry

    lax.fori_loop(1, n, greet, 0)
    lax.fori_loop(1, nh, greet_head, 0)

    q = q_ref[...]
    k = k_ref[...]
    u_src[0] = mm(v_ref[...], k, TN).astype(BF16)
    u_src[1] = (scale * mm(dy_ref[...], q, TN)).astype(BF16)

    pl.semaphore_wait(barrier, n - 1 + nh - 1)

    def when_owner(device):
        if n_own == n:
            return lambda body: body()
        return pl.when(device < n_own)

    def u_copy(target, source):
        return pltpu.make_async_remote_copy(
            src_ref=u_src.at[:, pl.ds(pl.multiple_of(target * rows, rows), rows)],
            dst_ref=u_all.at[source],
            send_sem=u_send.at[target],
            recv_sem=u_recv.at[source],
            device_id={"seq": target, "head": core},
            device_id_type=MESH,
        )

    def m_copy(target, source):
        return pltpu.make_async_remote_copy(
            src_ref=m_src,
            dst_ref=m_all.at[source],
            send_sem=m_send.at[target],
            recv_sem=m_recv.at[source],
            device_id={"seq": target, "head": core},
            device_id_type=MESH,
        )

    def s_copy(part, target, source):
        return pltpu.make_async_remote_copy(
            src_ref=s_src.at[part, target],
            dst_ref=s_all.at[part, pl.ds(pl.multiple_of(source * rows, rows), rows)],
            send_sem=s_send.at[part, target],
            recv_sem=s_recv.at[part, source],
            device_id={"seq": target, "head": core},
            device_id_type=MESH,
        )

    def send_u(i, carry):
        target = peer(i)

        @when_owner(target)
        def _():
            u_copy(target, me).start()

        return carry

    lax.fori_loop(1, n, send_u, 0)

    transition = normalized(raw_ref[0])
    eye = lax.broadcasted_iota(jnp.int32, (states, states), 0) == lax.broadcasted_iota(
        jnp.int32, (states, states), 1
    )
    diagonal = jnp.sum(jnp.where(eye, transition, 0.0), axis=0, keepdims=True)
    high = diagonal.astype(BF16).astype(F32)
    line = lax.broadcasted_iota(jnp.int32, (16, states), 0)
    m_src[0:states] = jnp.where(eye, 0.0, transition).astype(BF16)
    m_src[states : states + 16] = jnp.where(
        line == 0, high, jnp.where(line == 1, diagonal - high, 0.0)
    ).astype(BF16)

    def send_m(i, carry):
        target = peer(i)

        @when_owner(target)
        def _():
            m_copy(target, me).start()

        return carry

    lax.fori_loop(1, n, send_m, 0)

    @when_owner(me)
    def _():
        u_all[me] = u_src[:, pl.ds(pl.multiple_of(me * rows, rows), rows)]
        m_all[me] = m_src[...]

    causal = lax.broadcasted_iota(jnp.int32, (tokens, tokens), 0) >= lax.broadcasted_iota(
        jnp.int32, (tokens, tokens), 1
    )
    weights = jnp.where(causal, scale * mm(q, k, NT), 0.0).astype(BF16)
    av_acc[...] = mm(weights, v_ref[...], NN)
    ady_acc[...] = mm(weights, dy_ref[...], TN)
    gq = jnp.zeros((tokens, states), F32)
    gk = jnp.zeros((tokens, states), F32)
    for h in range(heads_here):
        span = slice(h * P_SIZE, (h + 1) * P_SIZE)
        dscore = mm(dy_ref[:, span], v_ref[:, span], NT)
        score_grad = jnp.where(causal, scale * dscore, 0.0).astype(BF16)
        gq += mm(score_grad, k, NN)
        gk += mm(score_grad, q, TN)
    gqk_part[0] = gq
    gqk_part[1] = gk

    def split(x):
        top = x.astype(BF16)
        return top, jnp.concatenate([top, (x - top.astype(F32)).astype(BF16)], axis=0)

    def step(lap, carry):
        x, y = carry
        late = n - 1 - lap
        x_low, x_pair = split(x)
        y_low, y_pair = split(y)
        s_src[0, lap] = x_low
        s_src[1, late] = y_low

        @pl.when(lap != me)
        def _():
            s_copy(0, lap, me).start()

        @pl.when(late != me)
        def _():
            s_copy(1, late, me).start()

        def diag(at):
            tail = m_all[at, states : states + 16].astype(F32)
            return tail[0:1] + tail[1:2]

        x_wide = mm(x_pair, m_all[lap, 0:states], NT)
        y_wide = mm(y_pair, m_all[late, 0:states], NN)
        x = x_wide[0:rows] + x_wide[rows:] + x * diag(lap) + u_all[lap, 0].astype(F32)
        y = y_wide[0:rows] + y_wide[rows:] + y * diag(late) + u_all[late, 1].astype(F32)
        return x, y

    @when_owner(me)
    def _():
        def arrive(i, carry):
            source = peer(i)
            u_copy(me, source).wait_recv()
            m_copy(me, source).wait_recv()
            return carry

        lax.fori_loop(1, n, arrive, 0)
        zero = jnp.zeros((rows, states), F32)
        lax.fori_loop(0, n, step, (zero, zero))
        own = pl.ds(pl.multiple_of(me * rows, rows), rows)
        s_all[0, own] = s_src[0, me]
        s_all[1, own] = s_src[1, me]

    def collect(i, carry):
        source = peer(i)

        @when_owner(source)
        def _():
            s_copy(0, me, source).wait_recv()
            s_copy(1, me, source).wait_recv()

        return carry

    lax.fori_loop(1, n, collect, 0)

    state_t = s_all[0]
    grad_t = s_all[1]
    gqk_part[0] += scale * mm(dy_ref[...], state_t, NN)
    gqk_part[1] += mm(v_ref[...], grad_t, NN)
    gt_part[...] = mm(grad_t, state_t, TN)

    share = tokens // nh
    row_share = states // nh

    def qk_copy(target, source):
        return pltpu.make_async_remote_copy(
            src_ref=gqk_part.at[:, pl.ds(pl.multiple_of(target * share, share), share)],
            dst_ref=gqk_all.at[source],
            send_sem=h_send.at[0, target],
            recv_sem=h_recv.at[0, source],
            device_id={"seq": me, "head": target},
            device_id_type=MESH,
        )

    def gt_copy(target, source):
        return pltpu.make_async_remote_copy(
            src_ref=gt_part.at[pl.ds(pl.multiple_of(target * row_share, row_share), row_share)],
            dst_ref=gt_all.at[source],
            send_sem=h_send.at[1, target],
            recv_sem=h_recv.at[1, source],
            device_id={"seq": me, "head": target},
            device_id_type=MESH,
        )

    def send_heads(i, carry):
        qk_copy(partner(i), core).start()
        gt_copy(partner(i), core).start()
        return carry

    lax.fori_loop(1, nh, send_heads, 0)

    out_ref[...] = (av_acc[...] + scale * mm(q, state_t, NT)).astype(BF16)
    gv_ref[...] = (ady_acc[...] + mm(k, grad_t, NT)).astype(BF16)

    own_share = pl.ds(pl.multiple_of(core * share, share), share)
    own_rows = pl.ds(pl.multiple_of(core * row_share, row_share), row_share)

    def add_heads(i, carry):
        gq_sum, gk_sum, gt_sum = carry
        source = partner(i)
        qk_copy(core, source).wait_recv()
        gt_copy(core, source).wait_recv()
        return (
            gq_sum + gqk_all[source, 0],
            gk_sum + gqk_all[source, 1],
            gt_sum + gt_all[source],
        )

    sums = (gqk_part[0, own_share], gqk_part[1, own_share], gt_part[own_rows])
    for i in range(1, nh):
        sums = add_heads(i, sums)
    gq_ref[...] = sums[0].astype(BF16)
    gk_ref[...] = sums[1].astype(BF16)
    gt_ref[...] = sums[2]

    def drain(i, carry):
        target = peer(i)

        @when_owner(target)
        def _():
            u_copy(target, me).wait_send()
            m_copy(target, me).wait_send()

        @when_owner(me)
        def _():
            s_copy(0, target, me).wait_send()
            s_copy(1, target, me).wait_send()

        return carry

    lax.fori_loop(1, n, drain, 0)

    def drain_heads(i, carry):
        qk_copy(partner(i), core).wait_send()
        gt_copy(partner(i), core).wait_send()
        return carry

    lax.fori_loop(1, nh, drain_heads, 0)


def per_device(queries, keys, values, out_grad, raw_trans):
    n = lax.axis_size("seq")
    nh = lax.axis_size("head")
    assert raw_trans.shape[0] == 1
    tokens, states = queries.shape
    cols = values.shape[1]
    rows = max(16, cols // n)
    n_own = cols // rows
    share = tokens // nh
    row_share = states // nh
    vmem = pl.BlockSpec(memory_space=pltpu.VMEM)
    outs = pl.pallas_call(
        functools.partial(kernel, n, nh, n_own, rows),
        out_shape=(
            jax.ShapeDtypeStruct((tokens, cols), BF16),
            jax.ShapeDtypeStruct((share, states), BF16),
            jax.ShapeDtypeStruct((share, states), BF16),
            jax.ShapeDtypeStruct((tokens, cols), BF16),
            jax.ShapeDtypeStruct((row_share, states), F32),
        ),
        in_specs=[vmem] * 5,
        out_specs=(vmem,) * 5,
        scratch_shapes=[
            pltpu.VMEM((2, cols, states), BF16),
            pltpu.VMEM((n, 2, rows, states), BF16),
            pltpu.VMEM((states + 16, states), BF16),
            pltpu.VMEM((n, states + 16, states), BF16),
            pltpu.VMEM((2, n, rows, states), BF16),
            pltpu.VMEM((2, cols, states), BF16),
            pltpu.VMEM((tokens, cols), F32),
            pltpu.VMEM((tokens, cols), F32),
            pltpu.VMEM((2, tokens, states), F32),
            pltpu.VMEM((nh, 2, share, states), F32),
            pltpu.VMEM((states, states), F32),
            pltpu.VMEM((nh, row_share, states), F32),
            pltpu.SemaphoreType.DMA((n,)),
            pltpu.SemaphoreType.DMA((n,)),
            pltpu.SemaphoreType.DMA((n,)),
            pltpu.SemaphoreType.DMA((n,)),
            pltpu.SemaphoreType.DMA((2, n)),
            pltpu.SemaphoreType.DMA((2, n)),
            pltpu.SemaphoreType.DMA((2, nh)),
            pltpu.SemaphoreType.DMA((2, nh)),
        ],
        compiler_params=pltpu.CompilerParams(
            collective_id=0, has_side_effects=True, vmem_limit_bytes=40 * 1024 * 1024
        ),
    )(queries, keys, values, out_grad, raw_trans)
    out, gq, gk, gv, gt = outs
    return out, gq, gk, gv, gt.reshape(row_share, 1, states)


def solution(mesh):
    in_specs = (
        P("seq", None),
        P("seq", None),
        P("seq", "head"),
        P("seq", "head"),
        P("seq", None, None),
    )
    out_specs = (
        P("seq", "head"),
        P(("seq", "head"), None),
        P(("seq", "head"), None),
        P("seq", "head"),
        P("head", "seq", None),
    )
    return jax.shard_map(
        per_device, mesh=mesh, in_specs=in_specs, out_specs=out_specs, check_vma=False
    )
```

```python
import functools
import math

import jax
import jax.numpy as jnp
from jax import lax
from jax.experimental import pallas as pl
from jax.experimental.pallas import tpu as pltpu
from jax.sharding import PartitionSpec as P

STATE_ROWS = 128
P_SIZE = 256
L = 256

F32 = jnp.float32
BF16 = jnp.bfloat16
MESH = pl.DeviceIdType.MESH
NN = (((1,), (0,)), ((), ()))
NT = (((1,), (1,)), ((), ()))
TN = (((0,), (0,)), ((), ()))


def mm(a, b, dims):
    return lax.dot_general(a, b, dims, preferred_element_type=F32)


def normalized(raw):
    rows, count = raw.shape
    vector = jnp.full((1, count), 1.0 / math.sqrt(count), F32)
    for _ in range(6):
        product = jnp.sum(raw * vector, axis=1, keepdims=True)
        returned = jnp.sum(raw * product, axis=0, keepdims=True)
        vector = returned / jnp.sqrt(jnp.sum(returned * returned, axis=1, keepdims=True))
    product = jnp.sum(raw * vector, axis=1, keepdims=True)
    return raw / jnp.sqrt(jnp.sum(product * product, axis=0, keepdims=True))


def split(x):
    top = x.astype(BF16)
    return top, (x - top.astype(F32)).astype(BF16)


def kernel(
    n,
    nh,
    group,
    chunks,
    q_hbm,
    k_hbm,
    v_hbm,
    dy_hbm,
    raw_hbm,
    out_ref,
    gq_ref,
    gk_ref,
    gv_ref,
    gt_ref,
    q_ref,
    k_ref,
    v_ref,
    dy_ref,
    raw_ref,
    u_src,
    u_all,
    m_src,
    m_all,
    e_src,
    e_all,
    tail_acc,
    s_src,
    s_all,
    av_acc,
    ady_acc,
    gqk_part,
    gqk_all,
    gt_part,
    gt_all,
    in_sem,
    u_send,
    u_recv,
    m_send,
    m_recv,
    e_send,
    e_recv,
    s_send,
    s_recv,
    h_send,
    h_recv,
):
    me = lax.axis_index("seq")
    core = lax.axis_index("head")
    place = lax.rem(me, group)
    plane = lax.div(me, group)
    planes = n // group
    half = planes // 2
    tokens, states = q_ref.shape
    cols = v_ref.shape[1]
    rows = cols // group
    piece = rows // chunks
    heads_here = cols // P_SIZE
    scale = 0.5 / math.sqrt(STATE_ROWS * L)

    def load(index, source, target):
        return pltpu.make_async_copy(source, target, in_sem.at[index])

    loads = [
        load(i, source, target)
        for i, (source, target) in enumerate(
            (
                (raw_hbm, raw_ref),
                (q_hbm, q_ref),
                (k_hbm, k_ref),
                (v_hbm, v_ref),
                (dy_hbm, dy_ref),
            )
        )
    ]
    for copy in loads:
        copy.start()

    def mate(i):
        return lax.rem(place + i, group)

    def partner(i):
        return lax.rem(core + i, nh)

    def at_place(j):
        return {"seq": plane * group + j, "head": core}

    def at_plane(z):
        return {"seq": z * group + place, "head": core}

    barrier = pltpu.get_barrier_semaphore()

    def signal(device):
        pl.semaphore_signal(barrier, inc=1, device_id=device, device_id_type=MESH)

    for i in range(1, group):
        signal(at_place(mate(i)))
    for i in range(1, nh):
        signal({"seq": me, "head": partner(i)})

    @pl.when(plane > 0)
    def _():
        signal(at_plane(plane - 1))

    @pl.when(plane < planes - 1)
    def _():
        signal(at_plane(plane + 1))

    for copy in loads:
        copy.wait()

    q = q_ref[...]
    k = k_ref[...]
    u_src[0] = mm(v_ref[...], k, TN).astype(BF16)
    u_src[1] = (scale * mm(dy_ref[...], q, TN)).astype(BF16)
    transition = normalized(raw_ref[0])
    eye = lax.broadcasted_iota(jnp.int32, (states, states), 0) == lax.broadcasted_iota(
        jnp.int32, (states, states), 1
    )
    diagonal = jnp.sum(jnp.where(eye, transition, 0.0), axis=0, keepdims=True)
    high = diagonal.astype(BF16).astype(F32)
    line = lax.broadcasted_iota(jnp.int32, (16, states), 0)
    m_src[0:states] = jnp.where(eye, 0.0, transition).astype(BF16)
    m_src[states : states + 16] = jnp.where(
        line == 0, high, jnp.where(line == 1, diagonal - high, 0.0)
    ).astype(BF16)

    above = lax.min(plane, 1)
    below = lax.min(planes - 1 - plane, 1)
    pl.semaphore_wait(barrier, group - 1 + nh - 1 + above + below)

    def slab(j):
        return pl.ds(pl.multiple_of(j * rows, rows), rows)

    def u_copy(target, source):
        return pltpu.make_async_remote_copy(
            src_ref=u_src.at[:, slab(target)],
            dst_ref=u_all.at[source],
            send_sem=u_send.at[target],
            recv_sem=u_recv.at[source],
            device_id=at_place(target),
            device_id_type=MESH,
        )

    def m_copy(target, source):
        return pltpu.make_async_remote_copy(
            src_ref=m_src,
            dst_ref=m_all.at[source],
            send_sem=m_send.at[target],
            recv_sem=m_recv.at[source],
            device_id=at_place(target),
            device_id_type=MESH,
        )

    def e_copy(part, chunk, target):
        span = pl.ds(chunk * piece, piece)
        return pltpu.make_async_remote_copy(
            src_ref=e_src.at[part, span],
            dst_ref=e_all.at[part, span],
            send_sem=e_send.at[part, chunk],
            recv_sem=e_recv.at[part, chunk],
            device_id=at_plane(target),
            device_id_type=MESH,
        )

    def s_copy(part, target, source):
        return pltpu.make_async_remote_copy(
            src_ref=s_src.at[part, target],
            dst_ref=s_all.at[part, slab(source)],
            send_sem=s_send.at[part, target],
            recv_sem=s_recv.at[part, source],
            device_id=at_place(target),
            device_id_type=MESH,
        )

    for i in range(1, group):
        m_copy(mate(i), place).start()
    for i in range(1, group):
        u_copy(mate(i), place).start()
    u_all[place] = u_src[:, slab(place)]
    m_all[place] = m_src[...]

    causal = lax.broadcasted_iota(jnp.int32, (tokens, tokens), 0) >= lax.broadcasted_iota(
        jnp.int32, (tokens, tokens), 1
    )
    weights = jnp.where(causal, scale * mm(q, k, NT), 0.0).astype(BF16)
    av_acc[...] = mm(weights, v_ref[...], NN)
    ady_acc[...] = mm(weights, dy_ref[...], TN)
    gq = jnp.zeros((tokens, states), F32)
    gk = jnp.zeros((tokens, states), F32)
    for h in range(heads_here):
        span = slice(h * P_SIZE, (h + 1) * P_SIZE)
        dscore = mm(dy_ref[:, span], v_ref[:, span], NT)
        score_grad = jnp.where(causal, scale * dscore, 0.0).astype(BF16)
        gq += mm(score_grad, k, NN)
        gk += mm(score_grad, q, TN)
    gqk_part[0] = gq
    gqk_part[1] = gk

    for i in range(1, group):
        m_copy(place, mate(i)).wait_recv()
    for i in range(1, group):
        u_copy(place, mate(i)).wait_recv()

    def advance(x, j, dims):
        count = x.shape[0]
        tail = m_all[j, states : states + 16].astype(F32)
        wide = mm(jnp.concatenate(split(x), axis=0), m_all[j, 0:states], dims)
        return wide[0:count] + wide[count:] + x * (tail[0:1] + tail[1:2])

    x = jnp.concatenate(
        [jnp.zeros((rows, states), F32), jnp.where(eye, 1.0, 0.0).astype(F32)], axis=0
    )
    y = jnp.zeros((rows, states), F32)
    for lap in range(group):
        late = group - 1 - lap
        if lap == 0:
            x_rows = u_all[0, 0].astype(F32)
            y = u_all[late, 1].astype(F32)
            product = advance(x[rows:], 0, NT)
        else:
            x = advance(jnp.concatenate([x_rows, product], axis=0), lap, NT)
            x_rows = x[0:rows] + u_all[lap, 0].astype(F32)
            product = x[rows:]
            y = advance(y, late, NN) + u_all[late, 1].astype(F32)
    tail_acc[0] = x_rows
    tail_acc[1] = y
    top, rest = split(product)
    spread = (jnp.concatenate([top, rest], axis=0), jnp.concatenate([top, rest], axis=1))

    def run(part):
        first = (plane == 0, plane == planes - 1)[part]
        final = (plane == planes - 1, plane == 0)[part]
        towards = (plane + 1, plane - 1)[part]
        dims = (NN, NT)[part]

        @pl.when(first)
        def _():
            e_src[part] = tail_acc[part].astype(BF16)
            e_all[part] = jnp.zeros((rows, states), BF16)
            if planes > 1:
                for chunk in range(chunks):
                    e_copy(part, chunk, towards).start()

        @pl.when(jnp.logical_not(first))
        def _():
            for chunk in range(chunks):
                e_copy(part, chunk, plane).wait_recv()

                @pl.when(jnp.logical_not(final))
                def _():
                    span = pl.ds(chunk * piece, piece)
                    entered = e_all[part, span]
                    left = mm(jnp.concatenate([entered, entered], axis=1), spread[part], dims)
                    e_src[part, span] = (left + tail_acc[part, span]).astype(BF16)
                    e_copy(part, chunk, towards).start()

        state = e_all[part].astype(F32)
        for lap in range(group):
            j = (lap, group - 1 - lap)[part]
            s_src[part, j] = state.astype(BF16)

            @pl.when(place != j)
            def _():
                s_copy(part, j, place).start()

            @pl.when(place == j)
            def _():
                s_all[part, slab(place)] = s_src[part, j]

            if lap < group - 1:
                state = advance(state, j, (NT, NN)[part]) + u_all[j, part].astype(F32)

    def collect(part):
        for i in range(1, group):
            s_copy(part, place, mate(i)).wait_recv()

    share = tokens // nh
    row_share = states // nh

    def qk_copy(target, source):
        return pltpu.make_async_remote_copy(
            src_ref=gqk_part.at[:, pl.ds(pl.multiple_of(target * share, share), share)],
            dst_ref=gqk_all.at[source],
            send_sem=h_send.at[0, target],
            recv_sem=h_recv.at[0, source],
            device_id={"seq": me, "head": target},
            device_id_type=MESH,
        )

    def gt_copy(target, source):
        return pltpu.make_async_remote_copy(
            src_ref=gt_part.at[pl.ds(pl.multiple_of(target * row_share, row_share), row_share)],
            dst_ref=gt_all.at[source],
            send_sem=h_send.at[1, target],
            recv_sem=h_recv.at[1, source],
            device_id={"seq": me, "head": target},
            device_id_type=MESH,
        )

    def small(part):
        if part == 0:
            gqk_part[0] += scale * mm(dy_ref[...], s_all[0], NN)
        else:
            gqk_part[1] += mm(v_ref[...], s_all[1], NN)

    def large(part):
        if part == 0:
            out_ref[...] = (av_acc[...] + scale * mm(q_ref[...], s_all[0], NT)).astype(BF16)
        else:
            gv_ref[...] = (ady_acc[...] + mm(k_ref[...], s_all[1], NT)).astype(BF16)

    def whole(part):
        other = 1 - part
        run(part)
        run(other)
        collect(part)
        small(part)
        large(part)
        collect(other)
        small(other)
        gt_part[...] = mm(s_all[1], s_all[0], TN)
        for i in range(1, nh):
            qk_copy(partner(i), core).start()
            gt_copy(partner(i), core).start()
        large(other)

    @pl.when(plane < half)
    def _():
        whole(0)

    @pl.when(plane >= half)
    def _():
        whole(1)

    own_share = pl.ds(pl.multiple_of(core * share, share), share)
    own_rows = pl.ds(pl.multiple_of(core * row_share, row_share), row_share)
    gq_sum = gqk_part[0, own_share]
    gk_sum = gqk_part[1, own_share]
    gt_sum = gt_part[own_rows]
    for i in range(1, nh):
        source = partner(i)
        qk_copy(core, source).wait_recv()
        gt_copy(core, source).wait_recv()
        gq_sum += gqk_all[source, 0]
        gk_sum += gqk_all[source, 1]
        gt_sum += gt_all[source]
    gq_ref[...] = gq_sum.astype(BF16)
    gk_ref[...] = gk_sum.astype(BF16)
    gt_ref[...] = gt_sum

    for i in range(1, group):
        target = mate(i)
        u_copy(target, place).wait_send()
        m_copy(target, place).wait_send()
        s_copy(0, target, place).wait_send()
        s_copy(1, target, place).wait_send()
    for i in range(1, nh):
        qk_copy(partner(i), core).wait_send()
        gt_copy(partner(i), core).wait_send()

    @pl.when(plane < planes - 1)
    def _():
        for chunk in range(chunks):
            e_copy(0, chunk, plane + 1).wait_send()

    @pl.when(plane > 0)
    def _():
        for chunk in range(chunks):
            e_copy(1, chunk, plane - 1).wait_send()


def store(*refs):
    count = len(refs) // 2
    sem = refs[-1]
    copies = [
        pltpu.make_async_copy(refs[i], refs[count + i], sem.at[i]) for i in range(count)
    ]
    for copy in copies:
        copy.start()
    for copy in copies:
        copy.wait()


def per_device(queries, keys, values, out_grad, raw_trans):
    n = lax.axis_size("seq")
    nh = lax.axis_size("head")
    assert raw_trans.shape[0] == 1
    tokens, states = queries.shape
    cols = values.shape[1]
    group = math.gcd(n, 4)
    rows = cols // group
    chunks = 2
    share = tokens // nh
    row_share = states // nh
    vmem = pl.BlockSpec(memory_space=pltpu.VMEM)
    anywhere = pl.BlockSpec(memory_space=pltpu.HBM)
    shapes = (
        jax.ShapeDtypeStruct((tokens, cols), BF16),
        jax.ShapeDtypeStruct((share, states), BF16),
        jax.ShapeDtypeStruct((share, states), BF16),
        jax.ShapeDtypeStruct((tokens, cols), BF16),
        jax.ShapeDtypeStruct((row_share, states), F32),
    )
    queries, keys, values, out_grad, raw_trans = (
        pltpu.with_memory_space_constraint(x, pltpu.HBM)
        for x in (queries, keys, values, out_grad, raw_trans)
    )
    outs = pl.pallas_call(
        functools.partial(kernel, n, nh, group, chunks),
        out_shape=shapes,
        in_specs=[anywhere] * 5,
        out_specs=(vmem,) * 5,
        scratch_shapes=[
            pltpu.VMEM((tokens, states), BF16),
            pltpu.VMEM((tokens, states), BF16),
            pltpu.VMEM((tokens, cols), BF16),
            pltpu.VMEM((tokens, cols), BF16),
            pltpu.VMEM((1, states, states), F32),
            pltpu.VMEM((2, cols, states), BF16),
            pltpu.VMEM((group, 2, rows, states), BF16),
            pltpu.VMEM((states + 16, states), BF16),
            pltpu.VMEM((group, states + 16, states), BF16),
            pltpu.VMEM((2, rows, states), BF16),
            pltpu.VMEM((2, rows, states), BF16),
            pltpu.VMEM((2, rows, states), F32),
            pltpu.VMEM((2, group, rows, states), BF16),
            pltpu.VMEM((2, cols, states), BF16),
            pltpu.VMEM((tokens, cols), F32),
            pltpu.VMEM((tokens, cols), F32),
            pltpu.VMEM((2, tokens, states), F32),
            pltpu.VMEM((nh, 2, share, states), F32),
            pltpu.VMEM((states, states), F32),
            pltpu.VMEM((nh, row_share, states), F32),
            pltpu.SemaphoreType.DMA((5,)),
            pltpu.SemaphoreType.DMA((group,)),
            pltpu.SemaphoreType.DMA((group,)),
            pltpu.SemaphoreType.DMA((group,)),
            pltpu.SemaphoreType.DMA((group,)),
            pltpu.SemaphoreType.DMA((2, chunks)),
            pltpu.SemaphoreType.DMA((2, chunks)),
            pltpu.SemaphoreType.DMA((2, group)),
            pltpu.SemaphoreType.DMA((2, group)),
            pltpu.SemaphoreType.DMA((2, nh)),
            pltpu.SemaphoreType.DMA((2, nh)),
        ],
        compiler_params=pltpu.CompilerParams(
            collective_id=0, has_side_effects=True, vmem_limit_bytes=32 * 1024 * 1024
        ),
    )(queries, keys, values, out_grad, raw_trans)
    out, gq, gk, gv, gt = pl.pallas_call(
        store,
        out_shape=shapes,
        in_specs=[vmem] * 5,
        out_specs=(anywhere,) * 5,
        scratch_shapes=[pltpu.SemaphoreType.DMA((5,))],
        compiler_params=pltpu.CompilerParams(vmem_limit_bytes=4 * 1024 * 1024),
    )(*outs)
    return out, gq, gk, gv, gt.reshape(row_share, 1, states)


def solution(mesh):
    in_specs = (
        P("seq", None),
        P("seq", None),
        P("seq", "head"),
        P("seq", "head"),
        P("seq", None, None),
    )
    out_specs = (
        P("seq", "head"),
        P(("seq", "head"), None),
        P(("seq", "head"), None),
        P("seq", "head"),
        P("head", "seq", None),
    )
    return jax.shard_map(
        per_device, mesh=mesh, in_specs=in_specs, out_specs=out_specs, check_vma=False
    )
```

```python
import functools
import math

import jax
import jax.numpy as jnp
from jax import lax
from jax.experimental import pallas as pl
from jax.experimental.pallas import tpu as pltpu
from jax.sharding import PartitionSpec as P

STATE_ROWS = 128
P_SIZE = 256
L = 256

F32 = jnp.float32
BF16 = jnp.bfloat16
MESH = pl.DeviceIdType.MESH
NN = (((1,), (0,)), ((), ()))
NT = (((1,), (1,)), ((), ()))
TN = (((0,), (0,)), ((), ()))


def mm(a, b, dims):
    return lax.dot_general(a, b, dims, preferred_element_type=F32)


def normalized(raw):
    rows, count = raw.shape
    vector = jnp.full((1, count), 1.0 / math.sqrt(count), F32)
    for _ in range(6):
        product = jnp.sum(raw * vector, axis=1, keepdims=True)
        returned = jnp.sum(raw * product, axis=0, keepdims=True)
        vector = returned / jnp.sqrt(jnp.sum(returned * returned, axis=1, keepdims=True))
    product = jnp.sum(raw * vector, axis=1, keepdims=True)
    return raw / jnp.sqrt(jnp.sum(product * product, axis=0, keepdims=True))


def split(x):
    top = x.astype(BF16)
    return top, (x - top.astype(F32)).astype(BF16)


def kernel(
    n,
    nh,
    group,
    chunks,
    q_hbm,
    k_hbm,
    v_hbm,
    dy_hbm,
    raw_hbm,
    out_ref,
    gq_ref,
    gk_ref,
    gv_ref,
    gt_ref,
    q_ref,
    k_ref,
    v_ref,
    dy_ref,
    raw_ref,
    u_src,
    u_all,
    m_src,
    m_all,
    e_src,
    e_all,
    prod,
    local,
    s_src,
    s_all,
    av_acc,
    ady_acc,
    gqk_part,
    gqk_all,
    gt_part,
    gt_all,
    in_sem,
    u_send,
    u_recv,
    m_send,
    m_recv,
    e_send,
    e_recv,
    s_send,
    s_recv,
    h_send,
    h_recv,
):
    me = lax.axis_index("seq")
    core = lax.axis_index("head")
    place = lax.rem(me, group)
    plane = lax.div(me, group)
    planes = n // group
    half = planes // 2
    tokens, states = q_ref.shape
    cols = v_ref.shape[1]
    rows = cols // group
    piece = rows // chunks
    heads_here = cols // P_SIZE
    scale = 0.5 / math.sqrt(STATE_ROWS * L)

    def load(index, source, target):
        return pltpu.make_async_copy(source, target, in_sem.at[index])

    loads = [
        load(i, source, target)
        for i, (source, target) in enumerate(
            (
                (raw_hbm, raw_ref),
                (q_hbm, q_ref),
                (k_hbm, k_ref),
                (v_hbm, v_ref),
                (dy_hbm, dy_ref),
            )
        )
    ]
    for copy in loads:
        copy.start()

    def mate(i):
        return lax.rem(place + i, group)

    def partner(i):
        return lax.rem(core + i, nh)

    def at_place(j):
        return {"seq": plane * group + j, "head": core}

    def at_plane(z):
        return {"seq": z * group + place, "head": core}

    barrier = pltpu.get_barrier_semaphore()

    def signal(device):
        pl.semaphore_signal(barrier, inc=1, device_id=device, device_id_type=MESH)

    for i in range(1, group):
        signal(at_place(mate(i)))
    for i in range(1, nh):
        signal({"seq": me, "head": partner(i)})

    @pl.when(plane > 0)
    def _():
        signal(at_plane(plane - 1))

    @pl.when(plane < planes - 1)
    def _():
        signal(at_plane(plane + 1))

    for copy in loads:
        copy.wait()

    q = q_ref[...]
    k = k_ref[...]
    u_src[0] = mm(v_ref[...], k, TN).astype(BF16)
    u_src[1] = (scale * mm(dy_ref[...], q, TN)).astype(BF16)
    transition = normalized(raw_ref[0])
    eye = lax.broadcasted_iota(jnp.int32, (states, states), 0) == lax.broadcasted_iota(
        jnp.int32, (states, states), 1
    )
    diagonal = jnp.sum(jnp.where(eye, transition, 0.0), axis=0, keepdims=True)
    high = diagonal.astype(BF16).astype(F32)
    line = lax.broadcasted_iota(jnp.int32, (16, states), 0)
    m_src[0:states] = jnp.where(eye, 0.0, transition).astype(BF16)
    m_src[states : states + 16] = jnp.where(
        line == 0, high, jnp.where(line == 1, diagonal - high, 0.0)
    ).astype(BF16)

    above = lax.min(plane, 1)
    below = lax.min(planes - 1 - plane, 1)
    pl.semaphore_wait(barrier, group - 1 + nh - 1 + above + below)

    def slab(j):
        return pl.ds(pl.multiple_of(j * rows, rows), rows)

    def bit(j, chunk):
        return pl.ds(pl.multiple_of(j * rows + chunk * piece, piece), piece)

    def u_copy(chunk, target, source):
        return pltpu.make_async_remote_copy(
            src_ref=u_src.at[:, bit(target, chunk)],
            dst_ref=u_all.at[source, :, pl.ds(chunk * piece, piece)],
            send_sem=u_send.at[chunk, target],
            recv_sem=u_recv.at[chunk, source],
            device_id=at_place(target),
            device_id_type=MESH,
        )

    def m_copy(target, source):
        return pltpu.make_async_remote_copy(
            src_ref=m_src,
            dst_ref=m_all.at[source],
            send_sem=m_send.at[target],
            recv_sem=m_recv.at[source],
            device_id=at_place(target),
            device_id_type=MESH,
        )

    def e_copy(part, chunk, target):
        span = pl.ds(chunk * piece, piece)
        return pltpu.make_async_remote_copy(
            src_ref=e_src.at[part, span],
            dst_ref=e_all.at[part, span],
            send_sem=e_send.at[part, chunk],
            recv_sem=e_recv.at[part, chunk],
            device_id=at_plane(target),
            device_id_type=MESH,
        )

    def s_copy(part, chunk, target, source):
        return pltpu.make_async_remote_copy(
            src_ref=s_src.at[part, target, pl.ds(chunk * piece, piece)],
            dst_ref=s_all.at[part, bit(source, chunk)],
            send_sem=s_send.at[part, chunk, target],
            recv_sem=s_recv.at[part, chunk, source],
            device_id=at_place(target),
            device_id_type=MESH,
        )

    for i in range(1, group):
        m_copy(mate(i), place).start()
    for chunk in range(chunks):
        for i in range(1, group):
            u_copy(chunk, mate(i), place).start()
    u_all[place] = u_src[:, slab(place)]
    m_all[place] = m_src[...]

    causal = lax.broadcasted_iota(jnp.int32, (tokens, tokens), 0) >= lax.broadcasted_iota(
        jnp.int32, (tokens, tokens), 1
    )
    weights = jnp.where(causal, scale * mm(q, k, NT), 0.0).astype(BF16)
    av_acc[...] = mm(weights, v_ref[...], NN)
    ady_acc[...] = mm(weights, dy_ref[...], TN)
    gq = jnp.zeros((tokens, states), F32)
    gk = jnp.zeros((tokens, states), F32)
    for h in range(heads_here):
        span = slice(h * P_SIZE, (h + 1) * P_SIZE)
        dscore = mm(dy_ref[:, span], v_ref[:, span], NT)
        score_grad = jnp.where(causal, scale * dscore, 0.0).astype(BF16)
        gq += mm(score_grad, k, NN)
        gk += mm(score_grad, q, TN)
    gqk_part[0] = gq
    gqk_part[1] = gk

    for i in range(1, group):
        m_copy(place, mate(i)).wait_recv()
    def advance(x, j, dims):
        count = x.shape[0]
        tail = m_all[j, states : states + 16].astype(F32)
        wide = mm(jnp.concatenate(split(x), axis=0), m_all[j, 0:states], dims)
        return wide[0:count] + wide[count:] + x * (tail[0:1] + tail[1:2])

    unit = jnp.where(eye, 1.0, 0.0).astype(F32)
    ahead = unit
    behind = unit
    for lap in range(group):
        span = slice(lap * states, (lap + 1) * states)
        ahead = advance(ahead, lap, NT)
        behind = advance(behind, group - 1 - lap, NN)
        prod[0, :, span] = jnp.concatenate(split(ahead), axis=0)
        prod[1, :, span] = jnp.concatenate(split(behind), axis=0)

    firsts = (plane == 0, plane == planes - 1)
    finals = (plane == planes - 1, plane == 0)
    towards = (plane + 1, plane - 1)

    for chunk in range(chunks):
        for i in range(1, group):
            u_copy(chunk, place, mate(i)).wait_recv()
        rest = pl.ds(chunk * piece, piece)
        x = u_all[0, 0, rest].astype(F32)
        y = u_all[group - 1, 1, rest].astype(F32)
        local[0, rest, 0:states] = x
        local[1, rest, 0:states] = y
        for lap in range(1, group):
            late = group - 1 - lap
            span = slice(lap * states, (lap + 1) * states)
            x = advance(x, lap, NT) + u_all[lap, 0, rest].astype(F32)
            y = advance(y, late, NN) + u_all[late, 1, rest].astype(F32)
            local[0, rest, span] = x
            local[1, rest, span] = y
        if planes > 1:
            for part, last in enumerate((x, y)):

                @pl.when(firsts[part])
                def _():
                    e_src[part, rest] = last.astype(BF16)
                    e_copy(part, chunk, towards[part]).start()

    for part in range(2):

        @pl.when(firsts[part])
        def _():
            e_all[part] = jnp.zeros((rows, states), BF16)

    edge = (group - 1) * states

    def run(part):
        for chunk in range(chunks):
            rest = pl.ds(chunk * piece, piece)

            @pl.when(jnp.logical_not(firsts[part]))
            def _():
                e_copy(part, chunk, plane).wait_recv()

            @pl.when(jnp.logical_not(jnp.logical_or(firsts[part], finals[part])))
            def _():
                entered = e_all[part, rest]
                left = mm(jnp.concatenate([entered, entered], axis=1), prod[part, :, edge:], NN)
                e_src[part, rest] = (left + local[part, rest, edge:]).astype(BF16)
                e_copy(part, chunk, towards[part]).start()

            entered = e_all[part, rest]
            doubled = jnp.concatenate([entered, entered], axis=1)
            for lap in range(group):
                j = (lap, group - 1 - lap)[part]
                if lap == 0:
                    state = entered
                else:
                    span = slice((lap - 1) * states, lap * states)
                    state = (mm(doubled, prod[part, :, span], NN) + local[part, rest, span]).astype(
                        BF16
                    )
                s_src[part, j, rest] = state

                @pl.when(place != j)
                def _():
                    s_copy(part, chunk, j, place).start()

                @pl.when(place == j)
                def _():
                    s_all[part, bit(place, chunk)] = state

    def collect(part):
        for chunk in range(chunks):
            for i in range(1, group):
                s_copy(part, chunk, place, mate(i)).wait_recv()

    share = tokens // nh
    row_share = states // nh

    def qk_copy(target, source):
        return pltpu.make_async_remote_copy(
            src_ref=gqk_part.at[:, pl.ds(pl.multiple_of(target * share, share), share)],
            dst_ref=gqk_all.at[source],
            send_sem=h_send.at[0, target],
            recv_sem=h_recv.at[0, source],
            device_id={"seq": me, "head": target},
            device_id_type=MESH,
        )

    def gt_copy(target, source):
        return pltpu.make_async_remote_copy(
            src_ref=gt_part.at[pl.ds(pl.multiple_of(target * row_share, row_share), row_share)],
            dst_ref=gt_all.at[source],
            send_sem=h_send.at[1, target],
            recv_sem=h_recv.at[1, source],
            device_id={"seq": me, "head": target},
            device_id_type=MESH,
        )

    def small(part):
        if part == 0:
            gqk_part[0] += scale * mm(dy_ref[...], s_all[0], NN)
        else:
            gqk_part[1] += mm(v_ref[...], s_all[1], NN)

    def large(part):
        if part == 0:
            out_ref[...] = (av_acc[...] + scale * mm(q_ref[...], s_all[0], NT)).astype(BF16)
        else:
            gv_ref[...] = (ady_acc[...] + mm(k_ref[...], s_all[1], NT)).astype(BF16)

    def whole(part):
        other = 1 - part
        run(part)
        run(other)
        collect(part)
        small(part)
        large(part)
        collect(other)
        small(other)
        gt_part[...] = mm(s_all[1], s_all[0], TN)
        for i in range(1, nh):
            qk_copy(partner(i), core).start()
            gt_copy(partner(i), core).start()
        large(other)

    @pl.when(plane < half)
    def _():
        whole(0)

    @pl.when(plane >= half)
    def _():
        whole(1)

    own_share = pl.ds(pl.multiple_of(core * share, share), share)
    own_rows = pl.ds(pl.multiple_of(core * row_share, row_share), row_share)
    gq_sum = gqk_part[0, own_share]
    gk_sum = gqk_part[1, own_share]
    gt_sum = gt_part[own_rows]
    for i in range(1, nh):
        source = partner(i)
        qk_copy(core, source).wait_recv()
        gt_copy(core, source).wait_recv()
        gq_sum += gqk_all[source, 0]
        gk_sum += gqk_all[source, 1]
        gt_sum += gt_all[source]
    gq_ref[...] = gq_sum.astype(BF16)
    gk_ref[...] = gk_sum.astype(BF16)
    gt_ref[...] = gt_sum

    for i in range(1, group):
        target = mate(i)
        m_copy(target, place).wait_send()
        for chunk in range(chunks):
            u_copy(chunk, target, place).wait_send()
            s_copy(0, chunk, target, place).wait_send()
            s_copy(1, chunk, target, place).wait_send()
    for i in range(1, nh):
        qk_copy(partner(i), core).wait_send()
        gt_copy(partner(i), core).wait_send()

    @pl.when(plane < planes - 1)
    def _():
        for chunk in range(chunks):
            e_copy(0, chunk, plane + 1).wait_send()

    @pl.when(plane > 0)
    def _():
        for chunk in range(chunks):
            e_copy(1, chunk, plane - 1).wait_send()


def store(*refs):
    count = len(refs) // 2
    sem = refs[-1]
    copies = [
        pltpu.make_async_copy(refs[i], refs[count + i], sem.at[i]) for i in range(count)
    ]
    for copy in copies:
        copy.start()
    for copy in copies:
        copy.wait()


def per_device(queries, keys, values, out_grad, raw_trans):
    n = lax.axis_size("seq")
    nh = lax.axis_size("head")
    assert raw_trans.shape[0] == 1
    tokens, states = queries.shape
    cols = values.shape[1]
    group = math.gcd(n, 4)
    rows = cols // group
    chunks = 2
    share = tokens // nh
    row_share = states // nh
    vmem = pl.BlockSpec(memory_space=pltpu.VMEM)
    anywhere = pl.BlockSpec(memory_space=pltpu.HBM)
    shapes = (
        jax.ShapeDtypeStruct((tokens, cols), BF16),
        jax.ShapeDtypeStruct((share, states), BF16),
        jax.ShapeDtypeStruct((share, states), BF16),
        jax.ShapeDtypeStruct((tokens, cols), BF16),
        jax.ShapeDtypeStruct((row_share, states), F32),
    )
    queries, keys, values, out_grad, raw_trans = (
        pltpu.with_memory_space_constraint(x, pltpu.HBM)
        for x in (queries, keys, values, out_grad, raw_trans)
    )
    outs = pl.pallas_call(
        functools.partial(kernel, n, nh, group, chunks),
        out_shape=shapes,
        in_specs=[anywhere] * 5,
        out_specs=(vmem,) * 5,
        scratch_shapes=[
            pltpu.VMEM((tokens, states), BF16),
            pltpu.VMEM((tokens, states), BF16),
            pltpu.VMEM((tokens, cols), BF16),
            pltpu.VMEM((tokens, cols), BF16),
            pltpu.VMEM((1, states, states), F32),
            pltpu.VMEM((2, cols, states), BF16),
            pltpu.VMEM((group, 2, rows, states), BF16),
            pltpu.VMEM((states + 16, states), BF16),
            pltpu.VMEM((group, states + 16, states), BF16),
            pltpu.VMEM((2, rows, states), BF16),
            pltpu.VMEM((2, rows, states), BF16),
            pltpu.VMEM((2, 2 * states, group * states), BF16),
            pltpu.VMEM((2, rows, group * states), F32),
            pltpu.VMEM((2, group, rows, states), BF16),
            pltpu.VMEM((2, cols, states), BF16),
            pltpu.VMEM((tokens, cols), F32),
            pltpu.VMEM((tokens, cols), F32),
            pltpu.VMEM((2, tokens, states), F32),
            pltpu.VMEM((nh, 2, share, states), F32),
            pltpu.VMEM((states, states), F32),
            pltpu.VMEM((nh, row_share, states), F32),
            pltpu.SemaphoreType.DMA((5,)),
            pltpu.SemaphoreType.DMA((chunks, group)),
            pltpu.SemaphoreType.DMA((chunks, group)),
            pltpu.SemaphoreType.DMA((group,)),
            pltpu.SemaphoreType.DMA((group,)),
            pltpu.SemaphoreType.DMA((2, chunks)),
            pltpu.SemaphoreType.DMA((2, chunks)),
            pltpu.SemaphoreType.DMA((2, chunks, group)),
            pltpu.SemaphoreType.DMA((2, chunks, group)),
            pltpu.SemaphoreType.DMA((2, nh)),
            pltpu.SemaphoreType.DMA((2, nh)),
        ],
        compiler_params=pltpu.CompilerParams(
            collective_id=0, has_side_effects=True, vmem_limit_bytes=32 * 1024 * 1024
        ),
    )(queries, keys, values, out_grad, raw_trans)
    out, gq, gk, gv, gt = pl.pallas_call(
        store,
        out_shape=shapes,
        in_specs=[vmem] * 5,
        out_specs=(anywhere,) * 5,
        scratch_shapes=[pltpu.SemaphoreType.DMA((5,))],
        compiler_params=pltpu.CompilerParams(vmem_limit_bytes=4 * 1024 * 1024),
    )(*outs)
    return out, gq, gk, gv, gt.reshape(row_share, 1, states)


def solution(mesh):
    in_specs = (
        P("seq", None),
        P("seq", None),
        P("seq", "head"),
        P("seq", "head"),
        P("seq", None, None),
    )
    out_specs = (
        P("seq", "head"),
        P(("seq", "head"), None),
        P(("seq", "head"), None),
        P("seq", "head"),
        P("head", "seq", None),
    )
    return jax.shard_map(
        per_device, mesh=mesh, in_specs=in_specs, out_specs=out_specs, check_vma=False
    )
```

```python
import functools
import math

import jax
import jax.numpy as jnp
from jax import lax
from jax.experimental import pallas as pl
from jax.experimental.pallas import tpu as pltpu
from jax.sharding import PartitionSpec as P

STATE_ROWS = 128
P_SIZE = 256
L = 256

F32 = jnp.float32
BF16 = jnp.bfloat16
MESH = pl.DeviceIdType.MESH
NN = (((1,), (0,)), ((), ()))
NT = (((1,), (1,)), ((), ()))
TN = (((0,), (0,)), ((), ()))


def mm(a, b, dims):
    return lax.dot_general(a, b, dims, preferred_element_type=F32)


def normalized(raw):
    rows, count = raw.shape
    vector = jnp.full((1, count), 1.0 / math.sqrt(count), F32)
    for _ in range(6):
        product = jnp.sum(raw * vector, axis=1, keepdims=True)
        returned = jnp.sum(raw * product, axis=0, keepdims=True)
        vector = returned / jnp.sqrt(jnp.sum(returned * returned, axis=1, keepdims=True))
    product = jnp.sum(raw * vector, axis=1, keepdims=True)
    return raw / jnp.sqrt(jnp.sum(product * product, axis=0, keepdims=True))


def split(x):
    top = x.astype(BF16)
    return top, (x - top.astype(F32)).astype(BF16)


def kernel(
    n,
    nh,
    group,
    chunks,
    q_hbm,
    k_hbm,
    v_hbm,
    dy_hbm,
    raw_hbm,
    out_ref,
    gq_ref,
    gk_ref,
    gv_ref,
    gt_ref,
    q_ref,
    k_ref,
    v_ref,
    dy_ref,
    raw_ref,
    u_src,
    u_all,
    m_src,
    m_all,
    a_src,
    a_all,
    e_src,
    e_all,
    prod,
    local,
    s_src,
    s_all,
    av_acc,
    ady_acc,
    gqk_part,
    gqk_all,
    gt_part,
    gt_all,
    in_sem,
    u_send,
    u_recv,
    m_send,
    m_recv,
    a_send,
    a_recv,
    e_send,
    e_recv,
    s_send,
    s_recv,
    h_send,
    h_recv,
):
    me = lax.axis_index("seq")
    core = lax.axis_index("head")
    place = lax.rem(me, group)
    plane = lax.div(me, group)
    planes = n // group
    half = planes // 2
    tokens, states = q_ref.shape
    cols = v_ref.shape[1]
    rows = cols // group
    piece = rows // chunks
    heads_here = cols // P_SIZE
    scale = 0.5 / math.sqrt(STATE_ROWS * L)

    def load(index, source, target):
        return pltpu.make_async_copy(source, target, in_sem.at[index])

    loads = [
        load(i, source, target)
        for i, (source, target) in enumerate(
            (
                (raw_hbm, raw_ref),
                (q_hbm, q_ref),
                (k_hbm, k_ref),
                (v_hbm, v_ref),
                (dy_hbm, dy_ref),
            )
        )
    ]
    for copy in loads:
        copy.start()

    def mate(i):
        return lax.rem(place + i, group)

    def partner(i):
        return lax.rem(core + i, nh)

    def at_place(j):
        return {"seq": plane * group + j, "head": core}

    def at_plane(z):
        return {"seq": z * group + place, "head": core}

    barrier = pltpu.get_barrier_semaphore()

    def signal(device):
        pl.semaphore_signal(barrier, inc=1, device_id=device, device_id_type=MESH)

    for i in range(1, group):
        signal(at_place(mate(i)))
    for i in range(1, nh):
        signal({"seq": me, "head": partner(i)})

    for i in range(1, planes):
        signal(at_plane(lax.rem(plane + i, planes)))

    for copy in loads:
        copy.wait()

    q = q_ref[...]
    k = k_ref[...]
    u_src[0] = mm(v_ref[...], k, TN).astype(BF16)
    u_src[1] = (scale * mm(dy_ref[...], q, TN)).astype(BF16)
    transition = normalized(raw_ref[0])
    eye = lax.broadcasted_iota(jnp.int32, (states, states), 0) == lax.broadcasted_iota(
        jnp.int32, (states, states), 1
    )
    line = lax.broadcasted_iota(jnp.int32, (16, states), 0)

    def encode(ref, full):
        diagonal = jnp.sum(jnp.where(eye, full, 0.0), axis=0, keepdims=True)
        high = diagonal.astype(BF16).astype(F32)
        ref[0:states] = jnp.where(eye, 0.0, full).astype(BF16)
        ref[states : states + 16] = jnp.where(
            line == 0, high, jnp.where(line == 1, diagonal - high, 0.0)
        ).astype(BF16)

    encode(m_src, transition)

    pl.semaphore_wait(barrier, group - 1 + nh - 1 + planes - 1)

    def slab(j):
        return pl.ds(pl.multiple_of(j * rows, rows), rows)

    def bit(j, chunk):
        return pl.ds(pl.multiple_of(j * rows + chunk * piece, piece), piece)

    def u_copy(chunk, target, source):
        return pltpu.make_async_remote_copy(
            src_ref=u_src.at[:, bit(target, chunk)],
            dst_ref=u_all.at[source, :, pl.ds(chunk * piece, piece)],
            send_sem=u_send.at[chunk, target],
            recv_sem=u_recv.at[chunk, source],
            device_id=at_place(target),
            device_id_type=MESH,
        )

    def m_copy(target, source):
        return pltpu.make_async_remote_copy(
            src_ref=m_src,
            dst_ref=m_all.at[source],
            send_sem=m_send.at[target],
            recv_sem=m_recv.at[source],
            device_id=at_place(target),
            device_id_type=MESH,
        )

    def a_copy(target, source):
        return pltpu.make_async_remote_copy(
            src_ref=a_src,
            dst_ref=a_all.at[source],
            send_sem=a_send.at[target],
            recv_sem=a_recv.at[source],
            device_id=at_plane(target),
            device_id_type=MESH,
        )

    def e_copy(part, chunk, target, source):
        span = pl.ds(chunk * piece, piece)
        return pltpu.make_async_remote_copy(
            src_ref=e_src.at[part, span],
            dst_ref=e_all.at[part, source, span],
            send_sem=e_send.at[part, chunk, target],
            recv_sem=e_recv.at[part, chunk, source],
            device_id=at_plane(target),
            device_id_type=MESH,
        )

    def s_copy(part, chunk, target, source):
        return pltpu.make_async_remote_copy(
            src_ref=s_src.at[part, target, pl.ds(chunk * piece, piece)],
            dst_ref=s_all.at[part, bit(source, chunk)],
            send_sem=s_send.at[part, chunk, target],
            recv_sem=s_recv.at[part, chunk, source],
            device_id=at_place(target),
            device_id_type=MESH,
        )

    for i in range(1, group):
        m_copy(mate(i), place).start()
    for chunk in range(chunks):
        for i in range(1, group):
            u_copy(chunk, mate(i), place).start()
    u_all[place] = u_src[:, slab(place)]
    m_all[place] = m_src[...]

    causal = lax.broadcasted_iota(jnp.int32, (tokens, tokens), 0) >= lax.broadcasted_iota(
        jnp.int32, (tokens, tokens), 1
    )
    weights = jnp.where(causal, scale * mm(q, k, NT), 0.0).astype(BF16)
    av_acc[...] = mm(weights, v_ref[...], NN)
    ady_acc[...] = mm(weights, dy_ref[...], TN)
    gq = jnp.zeros((tokens, states), F32)
    gk = jnp.zeros((tokens, states), F32)
    for h in range(heads_here):
        span = slice(h * P_SIZE, (h + 1) * P_SIZE)
        dscore = mm(dy_ref[:, span], v_ref[:, span], NT)
        score_grad = jnp.where(causal, scale * dscore, 0.0).astype(BF16)
        gq += mm(score_grad, k, NN)
        gk += mm(score_grad, q, TN)
    gqk_part[0] = gq
    gqk_part[1] = gk

    for i in range(1, group):
        m_copy(place, mate(i)).wait_recv()
    def apply(x, ref, j, dims):
        count = x.shape[0]
        tail = ref[j, states : states + 16].astype(F32)
        wide = mm(jnp.concatenate(split(x), axis=0), ref[j, 0:states], dims)
        return wide[0:count] + wide[count:] + x * (tail[0:1] + tail[1:2])

    def advance(x, j, dims):
        return apply(x, m_all, j, dims)

    unit = jnp.where(eye, 1.0, 0.0).astype(F32)
    ahead = unit
    behind = unit
    for lap in range(group):
        span = slice(lap * states, (lap + 1) * states)
        ahead = advance(ahead, lap, NT)
        behind = advance(behind, group - 1 - lap, NN)
        prod[0, :, span] = jnp.concatenate(split(ahead), axis=0)
        prod[1, :, span] = jnp.concatenate(split(behind), axis=0)

    encode(a_src, behind)
    for i in range(1, planes):
        a_copy(lax.rem(plane + i, planes), plane).start()

    for chunk in range(chunks):
        for i in range(1, group):
            u_copy(chunk, place, mate(i)).wait_recv()
        rest = pl.ds(chunk * piece, piece)
        x = u_all[0, 0, rest].astype(F32)
        y = u_all[group - 1, 1, rest].astype(F32)
        local[0, rest, 0:states] = x
        local[1, rest, 0:states] = y
        for lap in range(1, group):
            late = group - 1 - lap
            span = slice(lap * states, (lap + 1) * states)
            x = advance(x, lap, NT) + u_all[lap, 0, rest].astype(F32)
            y = advance(y, late, NN) + u_all[late, 1, rest].astype(F32)
            local[0, rest, span] = x
            local[1, rest, span] = y
        e_src[0, rest] = x.astype(BF16)
        e_src[1, rest] = y.astype(BF16)
        for i in range(1, planes):

            @pl.when(plane + i < planes)
            def _():
                e_copy(0, chunk, plane + i, plane).start()

            @pl.when(plane - i >= 0)
            def _():
                e_copy(1, chunk, plane - i, plane).start()

    for i in range(1, planes):
        a_copy(plane, lax.rem(plane + i, planes)).wait_recv()

    def run(part):
        for chunk in range(chunks):
            rest = pl.ds(chunk * piece, piece)

            def hop(i, held):
                source = (i, planes - 1 - i)[part]
                e_copy(part, chunk, plane, source).wait_recv()
                moved = apply(held, a_all, source, (NT, NN)[part])
                return moved + e_all[part, source, rest].astype(F32)

            entered = lax.fori_loop(
                0,
                (plane, planes - 1 - plane)[part],
                hop,
                jnp.zeros((piece, states), F32),
            ).astype(BF16)
            doubled = jnp.concatenate([entered, entered], axis=1)
            for lap in range(group):
                j = (lap, group - 1 - lap)[part]
                if lap == 0:
                    state = entered
                else:
                    span = slice((lap - 1) * states, lap * states)
                    state = (mm(doubled, prod[part, :, span], NN) + local[part, rest, span]).astype(
                        BF16
                    )
                s_src[part, j, rest] = state

                @pl.when(place != j)
                def _():
                    s_copy(part, chunk, j, place).start()

                @pl.when(place == j)
                def _():
                    s_all[part, bit(place, chunk)] = state

    def collect(part):
        for chunk in range(chunks):
            for i in range(1, group):
                s_copy(part, chunk, place, mate(i)).wait_recv()

    share = tokens // nh
    row_share = states // nh

    def qk_copy(target, source):
        return pltpu.make_async_remote_copy(
            src_ref=gqk_part.at[:, pl.ds(pl.multiple_of(target * share, share), share)],
            dst_ref=gqk_all.at[source],
            send_sem=h_send.at[0, target],
            recv_sem=h_recv.at[0, source],
            device_id={"seq": me, "head": target},
            device_id_type=MESH,
        )

    def gt_copy(target, source):
        return pltpu.make_async_remote_copy(
            src_ref=gt_part.at[pl.ds(pl.multiple_of(target * row_share, row_share), row_share)],
            dst_ref=gt_all.at[source],
            send_sem=h_send.at[1, target],
            recv_sem=h_recv.at[1, source],
            device_id={"seq": me, "head": target},
            device_id_type=MESH,
        )

    def small(part):
        if part == 0:
            gqk_part[0] += scale * mm(dy_ref[...], s_all[0], NN)
        else:
            gqk_part[1] += mm(v_ref[...], s_all[1], NN)

    def large(part):
        if part == 0:
            out_ref[...] = (av_acc[...] + scale * mm(q_ref[...], s_all[0], NT)).astype(BF16)
        else:
            gv_ref[...] = (ady_acc[...] + mm(k_ref[...], s_all[1], NT)).astype(BF16)

    def whole(part):
        other = 1 - part
        run(part)
        run(other)
        collect(part)
        small(part)
        large(part)
        collect(other)
        small(other)
        gt_part[...] = mm(s_all[1], s_all[0], TN)
        for i in range(1, nh):
            qk_copy(partner(i), core).start()
            gt_copy(partner(i), core).start()
        large(other)

    @pl.when(plane < half)
    def _():
        whole(0)

    @pl.when(plane >= half)
    def _():
        whole(1)

    own_share = pl.ds(pl.multiple_of(core * share, share), share)
    own_rows = pl.ds(pl.multiple_of(core * row_share, row_share), row_share)
    gq_sum = gqk_part[0, own_share]
    gk_sum = gqk_part[1, own_share]
    gt_sum = gt_part[own_rows]
    for i in range(1, nh):
        source = partner(i)
        qk_copy(core, source).wait_recv()
        gt_copy(core, source).wait_recv()
        gq_sum += gqk_all[source, 0]
        gk_sum += gqk_all[source, 1]
        gt_sum += gt_all[source]
    gq_ref[...] = gq_sum.astype(BF16)
    gk_ref[...] = gk_sum.astype(BF16)
    gt_ref[...] = gt_sum

    for i in range(1, group):
        target = mate(i)
        m_copy(target, place).wait_send()
        for chunk in range(chunks):
            u_copy(chunk, target, place).wait_send()
            s_copy(0, chunk, target, place).wait_send()
            s_copy(1, chunk, target, place).wait_send()
    for i in range(1, nh):
        qk_copy(partner(i), core).wait_send()
        gt_copy(partner(i), core).wait_send()

    for i in range(1, planes):
        a_copy(lax.rem(plane + i, planes), plane).wait_send()

        @pl.when(plane + i < planes)
        def _():
            for chunk in range(chunks):
                e_copy(0, chunk, plane + i, plane).wait_send()

        @pl.when(plane - i >= 0)
        def _():
            for chunk in range(chunks):
                e_copy(1, chunk, plane - i, plane).wait_send()


def store(*refs):
    count = len(refs) // 2
    sem = refs[-1]
    copies = [
        pltpu.make_async_copy(refs[i], refs[count + i], sem.at[i]) for i in range(count)
    ]
    for copy in copies:
        copy.start()
    for copy in copies:
        copy.wait()


def per_device(queries, keys, values, out_grad, raw_trans):
    n = lax.axis_size("seq")
    nh = lax.axis_size("head")
    assert raw_trans.shape[0] == 1
    tokens, states = queries.shape
    cols = values.shape[1]
    group = math.gcd(n, 4)
    rows = cols // group
    chunks = 2
    share = tokens // nh
    row_share = states // nh
    vmem = pl.BlockSpec(memory_space=pltpu.VMEM)
    anywhere = pl.BlockSpec(memory_space=pltpu.HBM)
    shapes = (
        jax.ShapeDtypeStruct((tokens, cols), BF16),
        jax.ShapeDtypeStruct((share, states), BF16),
        jax.ShapeDtypeStruct((share, states), BF16),
        jax.ShapeDtypeStruct((tokens, cols), BF16),
        jax.ShapeDtypeStruct((row_share, states), F32),
    )
    queries, keys, values, out_grad, raw_trans = (
        pltpu.with_memory_space_constraint(x, pltpu.HBM)
        for x in (queries, keys, values, out_grad, raw_trans)
    )
    outs = pl.pallas_call(
        functools.partial(kernel, n, nh, group, chunks),
        out_shape=shapes,
        in_specs=[anywhere] * 5,
        out_specs=(vmem,) * 5,
        scratch_shapes=[
            pltpu.VMEM((tokens, states), BF16),
            pltpu.VMEM((tokens, states), BF16),
            pltpu.VMEM((tokens, cols), BF16),
            pltpu.VMEM((tokens, cols), BF16),
            pltpu.VMEM((1, states, states), F32),
            pltpu.VMEM((2, cols, states), BF16),
            pltpu.VMEM((group, 2, rows, states), BF16),
            pltpu.VMEM((states + 16, states), BF16),
            pltpu.VMEM((group, states + 16, states), BF16),
            pltpu.VMEM((states + 16, states), BF16),
            pltpu.VMEM((n // group, states + 16, states), BF16),
            pltpu.VMEM((2, rows, states), BF16),
            pltpu.VMEM((2, n // group, rows, states), BF16),
            pltpu.VMEM((2, 2 * states, group * states), BF16),
            pltpu.VMEM((2, rows, group * states), F32),
            pltpu.VMEM((2, group, rows, states), BF16),
            pltpu.VMEM((2, cols, states), BF16),
            pltpu.VMEM((tokens, cols), F32),
            pltpu.VMEM((tokens, cols), F32),
            pltpu.VMEM((2, tokens, states), F32),
            pltpu.VMEM((nh, 2, share, states), F32),
            pltpu.VMEM((states, states), F32),
            pltpu.VMEM((nh, row_share, states), F32),
            pltpu.SemaphoreType.DMA((5,)),
            pltpu.SemaphoreType.DMA((chunks, group)),
            pltpu.SemaphoreType.DMA((chunks, group)),
            pltpu.SemaphoreType.DMA((group,)),
            pltpu.SemaphoreType.DMA((group,)),
            pltpu.SemaphoreType.DMA((n // group,)),
            pltpu.SemaphoreType.DMA((n // group,)),
            pltpu.SemaphoreType.DMA((2, chunks, n // group)),
            pltpu.SemaphoreType.DMA((2, chunks, n // group)),
            pltpu.SemaphoreType.DMA((2, chunks, group)),
            pltpu.SemaphoreType.DMA((2, chunks, group)),
            pltpu.SemaphoreType.DMA((2, nh)),
            pltpu.SemaphoreType.DMA((2, nh)),
        ],
        compiler_params=pltpu.CompilerParams(
            collective_id=0, has_side_effects=True, vmem_limit_bytes=32 * 1024 * 1024
        ),
    )(queries, keys, values, out_grad, raw_trans)
    out, gq, gk, gv, gt = pl.pallas_call(
        store,
        out_shape=shapes,
        in_specs=[vmem] * 5,
        out_specs=(anywhere,) * 5,
        scratch_shapes=[pltpu.SemaphoreType.DMA((5,))],
        compiler_params=pltpu.CompilerParams(vmem_limit_bytes=4 * 1024 * 1024),
    )(*outs)
    return out, gq, gk, gv, gt.reshape(row_share, 1, states)


def solution(mesh):
    in_specs = (
        P("seq", None),
        P("seq", None),
        P("seq", "head"),
        P("seq", "head"),
        P("seq", None, None),
    )
    out_specs = (
        P("seq", "head"),
        P(("seq", "head"), None),
        P(("seq", "head"), None),
        P("seq", "head"),
        P("head", "seq", None),
    )
    return jax.shard_map(
        per_device, mesh=mesh, in_specs=in_specs, out_specs=out_specs, check_vma=False
    )
```
